32 devices in a mesh: seq: 8 (over y, x, core), sub: 4 (over z).
Axes of the slice: x: 2, y: 2, z: 4, core: 2. Of those that a mesh axis runs over, the one named last changes fastest.
Arguments:
- query_rows: bfloat16 [8192, 1120], P(('seq', 'sub')), may hold values from -6 to 6
- key_rows: bfloat16 [8192, 1120], P(('seq', 'sub')), may hold values from -6 to 6
- value_rows: bfloat16 [8192, 1120], P(('seq', 'sub')), may hold values from -6 to 6
- query_tangent: bfloat16 [8192, 1120], P(('seq', 'sub')), may hold values from -6 to 6
- key_tangent: bfloat16 [8192, 1120], P(('seq', 'sub')), may hold values from -6 to 6
- value_tangent: bfloat16 [8192, 1120], P(('seq', 'sub')), may hold values from -6 to 6
- teacher: bfloat16 [8192, 2240], P(('seq', 'sub')), may hold values from -64 to 64
- out_weight: bfloat16 [1120, 2240], replicated, may hold values from -0.1875 to 0.1875
- norm_gain: float32 [1120], replicated, may hold values from 0.1 to 1.9
- clip_length: int32 [1], replicated, may hold values from 4096 to 8192
- block_mask: int32 [128], P(('seq', 'sub')), may hold values 0 or 1
Outputs:
- residual: bfloat16 [8192, 2240], P(('seq', 'sub'))
- grad_query: bfloat16 [8192, 1120], P(('seq', 'sub'))
- grad_key: bfloat16 [8192, 1120], P(('seq', 'sub'))
- grad_value: bfloat16 [8192, 1120], P(('seq', 'sub'))
The draws below stay inside these ranges and needn't reach their ends.
All inputs are finite; a program needn't handle non-finite values. No bound on the sum of `block_mask` on one device may be relied on, other than what follows from the above.
Results may differ from the reference program's by a relative error of at most 0.007.
Values may be sent and summed in bfloat16 or wider, within the bound.
A program may use at most 64 MiB of HBM per device.

```python
import jax
import jax.numpy as jnp
from jax import lax

D = 2240
H = 10
E = 112
BLK = 64
TOKENS = 8192
NBLK = 128


def draw_teacher(key, part):
    level_key = jax.random.fold_in(key, 11)
    entry_key = jax.random.fold_in(key, 12)
    groups = (TOKENS + 255) // 256
    levels = 6.0 * jnp.exp(jax.random.uniform(level_key, (groups,), jnp.float32, -1.0, 1.0))
    entries = jnp.clip(jax.random.normal(entry_key, (TOKENS, D), jnp.float32), -3.5, 3.5)
    row_group = jnp.arange(TOKENS, dtype=jnp.int32) // 256
    return (levels[row_group][:, None] * entries).astype(jnp.bfloat16)


def touch_ends(drawn, stream_key, low, largest):
    spot = [jax.random.randint(jax.random.fold_in(stream_key, axis), (), 0, length) for axis, length in enumerate(drawn.shape)]
    longest = drawn.shape.index(max(drawn.shape))
    next_to = spot[:longest] + [(spot[longest] + 1) % drawn.shape[longest]] + spot[longest + 1:]
    return drawn.at[tuple(spot)].set(low).at[tuple(next_to)].set(largest)


def block_levels(own_key, shape, split, least, largest):
    def one(axis_at, parts):
        steps = jax.random.uniform(jax.random.fold_in(jax.random.fold_in(own_key, 6), axis_at), (parts,), jnp.float32, least / len(split), largest / len(split))
        return jnp.repeat(jnp.exp(steps), shape[axis_at] // parts).reshape((-1,) + (1,) * (len(shape) - axis_at - 1))

    gain = one(*split[0])
    for cut in split[1:]:
        gain = gain * one(*cut)
    return gain


def normal_values(key, extent, spread, reach, cuts=(), kind=jnp.bfloat16):
    factor_of = block_levels(key, extent, cuts, -0.22, 0.18) if cuts else 1.0
    values = jax.random.normal(key, extent, jnp.float32) * spread * factor_of
    return jnp.minimum(jnp.maximum(values, -reach), reach).astype(kind)


def setup_inputs(seed: int = 0) -> dict:
    key_of = jax.random.split(jax.random.key(seed), 12)
    query_rows = normal_values(key_of[0], (TOKENS, H * E), 1.0, 6.0, ((0, 32),))
    key_rows = normal_values(key_of[1], (TOKENS, H * E), 1.0, 6.0, ((0, 32),))
    value_rows = normal_values(key_of[2], (TOKENS, H * E), 1.0, 6.0, ((0, 32),))
    query_tangent = normal_values(key_of[3], (TOKENS, H * E), 1.0, 6.0, ((0, 32),))
    key_tangent = normal_values(key_of[4], (TOKENS, H * E), 1.0, 6.0, ((0, 32),))
    value_tangent = normal_values(key_of[5], (TOKENS, H * E), 1.0, 6.0, ((0, 32),))
    teacher = draw_teacher(jax.random.fold_in(key_of[11], 71), 0)
    out_weight = normal_values(key_of[7], (H * E, D), (H * E) ** -0.5, 0.1875)
    norm_gain = jnp.clip(1.0 + 0.18 * jax.random.normal(key_of[8], (H * E,), jnp.float32), 0.1, 1.9)
    clip_length = jax.random.randint(key_of[9], (1,), TOKENS // 2, TOKENS + 1).astype(jnp.int32)
    block_mask = touch_ends((jax.random.randint(key_of[10], (NBLK,), 0, 8) < 7).astype(jnp.int32), jax.random.fold_in(key_of[10], 1), 0, 1)
    return dict(query_rows=query_rows, key_rows=key_rows, value_rows=value_rows, query_tangent=query_tangent, key_tangent=key_tangent, value_tangent=value_tangent, teacher=teacher, out_weight=out_weight, norm_gain=norm_gain, clip_length=clip_length, block_mask=block_mask)


def split_heads(matrix):
    return matrix.reshape(matrix.shape[0], H, E)

def norm_back(unnorm, scale_inv, weighted):
    inner_mean = lax.optimization_barrier(jnp.mean(unnorm * weighted, axis=-1, keepdims=True))
    return scale_inv * weighted - unnorm * (scale_inv * scale_inv * scale_inv) * inner_mean

def reference(query_rows, key_rows, value_rows, query_tangent, key_tangent, value_tangent, teacher, out_weight, norm_gain, clip_length, block_mask):
    f32 = jnp.float32
    bf16 = jnp.bfloat16
    seq_total = query_rows.shape[0]
    position = jnp.arange(seq_total, dtype=jnp.int32)
    block_flags = jnp.repeat(block_mask, BLK)
    valid_rows = jnp.where((position < clip_length[0]) & (block_flags == 1), 1.0, 0.0).astype(f32)[:, None]
    key_vals = key_rows.astype(f32)
    key_feat = (valid_rows * jnp.maximum(key_vals, 0.0)).astype(bf16)
    key_slope = valid_rows * jnp.where(key_vals > 0, 1.0, 0.0).astype(f32)
    key_dot = (key_slope * key_tangent.astype(f32)).astype(bf16)
    value_heads = split_heads(value_rows).astype(f32)
    feat_keys = split_heads(key_feat).astype(f32)
    state = jnp.einsum('the,thf->hef', feat_keys, value_heads).astype(bf16)
    state_dot = (jnp.einsum('the,thf->hef', split_heads(key_dot).astype(f32), value_heads) + jnp.einsum('the,thf->hef', feat_keys, split_heads(value_tangent).astype(f32))).astype(bf16)
    query_vals = query_rows.astype(f32)
    query_feat = jnp.maximum(query_vals, 0.0).astype(bf16)
    query_slope = jnp.where(query_vals > 0, 1.0, 0.0).astype(f32)
    query_dot = (query_slope * query_tangent.astype(f32)).astype(bf16)
    feat_heads = split_heads(query_feat).astype(f32)
    state_full = state.astype(f32)
    unnorm = jnp.einsum('the,hef->thf', feat_heads, state_full)
    unnorm_dot = jnp.einsum('the,hef->thf', split_heads(query_dot).astype(f32), state_full) + jnp.einsum('the,hef->thf', feat_heads, state_dot.astype(f32))
    gain_heads = norm_gain.reshape(H, E)
    scale_inv = lax.rsqrt(lax.optimization_barrier(jnp.mean(unnorm * unnorm, axis=-1, keepdims=True)) + 1e-06)
    normed_dot = (gain_heads * norm_back(unnorm, scale_inv, unnorm_dot)).astype(bf16).reshape(seq_total, H * E)
    velocity = jnp.dot(normed_dot, out_weight, preferred_element_type=f32)
    residual = (velocity - teacher.astype(f32)).astype(bf16)
    normed_grad = jnp.dot(residual, out_weight.T, preferred_element_type=f32)
    unnorm_grad = norm_back(unnorm, scale_inv, gain_heads * split_heads(normed_grad)).astype(bf16)
    grad_heads = unnorm_grad.astype(f32)
    state_grad = jnp.einsum('the,thf->hef', feat_heads, grad_heads).astype(bf16).astype(f32)
    grad_query = (query_slope * jnp.einsum('thf,hef->the', grad_heads, state_full).reshape(seq_total, H * E)).astype(bf16)
    grad_key = (key_slope * jnp.einsum('thf,hef->the', value_heads, state_grad).reshape(seq_total, H * E)).astype(bf16)
    grad_value = jnp.einsum('the,hef->thf', feat_keys, state_grad).reshape(seq_total, H * E).astype(bf16)
    return (residual, grad_query, grad_key, grad_value)
```

```python
import functools

import jax
import jax.numpy as jnp
from jax import lax
from jax.experimental import pallas as pl
from jax.experimental.pallas import tpu as pltpu
from jax.sharding import PartitionSpec as P

H = 10
E = 112
BLK = 64


MESH = pl.DeviceIdType.MESH
LANES = 128
VMEM_BYTES = 67043328
FINISH_VMEM = 16 << 20
f32 = jnp.float32
bf16 = jnp.bfloat16


def norm_back(unnorm, scale_inv, weighted):
    inner_mean = jnp.mean(unnorm * weighted, axis=0, keepdims=True)
    return scale_inv * weighted - unnorm * (scale_inv * scale_inv * scale_inv) * inner_mean


def dot(left, right, over):
    return lax.dot_general(left, right, ((over[:1], over[1:]), ((), ())), preferred_element_type=f32)


class Where:
    def __init__(self, chips, depth):
        seq = lax.axis_index("seq")
        self.sub = lax.axis_index("sub")
        self.depth = depth
        self.chips = chips
        self.core = lax.rem(seq, 2)
        self.chip = (seq // 2) * depth + self.sub
        self.partner = (seq + 1 - 2 * self.core, self.sub)

    def peer(self, index):
        return (index // self.depth) * 2 + self.core, lax.rem(index, self.depth)

    def ahead(self, step):
        return lax.rem(self.chip + step, self.chips)

    def behind(self, step):
        return lax.rem(self.chip + self.chips - step, self.chips)


def greet(at):
    barrier = pltpu.get_barrier_semaphore()
    pl.semaphore_signal(barrier, inc=1, device_id=at.partner, device_id_type=MESH)

    @pl.loop(1, at.chips)
    def _(step):
        pl.semaphore_signal(
            barrier, inc=1, device_id=at.peer(at.ahead(step)), device_id_type=MESH
        )


def all_total(at, piece, wide, near, sent, out, half, mine, parts, sems, between=None, after=None):
    s0, r0, s1, r1, s2, r2, s3, r3 = sems
    core, chip, chips = at.core, at.chip, at.chips

    def copy(src, dst, send, recv, to):
        return pltpu.make_async_remote_copy(
            src_ref=src,
            dst_ref=dst,
            send_sem=send,
            recv_sem=recv,
            device_id=to,
            device_id_type=MESH,
        )

    def rows(index, side=None):
        base = index if side is None else side * chips + index
        return pl.ds(pl.multiple_of(base * piece, 16), piece)

    def scatter(index, slot):
        return copy(
            mine.at[rows(index)], parts.at[rows(slot)], s1.at[index], r1.at[slot], at.peer(index)
        )

    def gather(index, slot):
        return copy(
            out.at[rows(chip, core)],
            out.at[rows(slot, core)],
            s2.at[index],
            r2.at[slot],
            at.peer(index),
        )

    def forward(index, side):
        return copy(
            out.at[rows(index, core)],
            out.at[rows(index, side)],
            s3.at[index],
            r3.at[index],
            at.partner,
        )

    size = wide.shape[0]
    for block in range(wide.shape[1] // LANES):
        lanes = wide[:, block * LANES : (block + 1) * LANES]
        near[block * size : (block + 1) * size, :] = lanes
        sent[block * size : (block + 1) * size, :] = lanes.astype(bf16)
    used = size * (wide.shape[1] // LANES)
    if used < near.shape[0]:
        near[used:, :] = jnp.zeros((near.shape[0] - used, LANES), f32)
        sent[used:, :] = jnp.zeros((near.shape[0] - used, LANES), bf16)

    other = pl.ds(pl.multiple_of((1 - core) * (chips * piece), 16), chips * piece)
    swap = copy(sent.at[other], half, s0, r0, at.partner)
    swap.start()
    if between is not None:
        between()
    swap.wait()

    def pair(index):
        return near[rows(index, core), :] + half[rows(index), :].astype(f32)

    @pl.loop(1, chips)
    def _(step):
        index = at.ahead(step)
        mine[rows(index), :] = pair(index).astype(bf16)
        scatter(index, chip).start()

    if after is not None:
        after()

    def add(step, acc):
        index = at.behind(step)
        scatter(index, index).wait_recv()
        return acc + parts[rows(index), :].astype(f32)

    out[rows(chip, core), :] = lax.fori_loop(1, chips, add, pair(chip)).astype(bf16)

    @pl.loop(1, chips)
    def _(step):
        gather(at.ahead(step), chip).start()

    forward(chip, core).start()

    @pl.loop(1, chips)
    def _(step):
        index = at.behind(step)
        gather(index, index).wait_recv()
        forward(index, core).start()

    @pl.loop(1, chips)
    def _(step):
        index = at.ahead(step)
        scatter(index, chip).wait_send()
        gather(index, chip).wait_send()

    @pl.loop(0, chips)
    def _(step):
        index = at.behind(step)
        forward(index, 1 - core).wait_recv()
        forward(index, core).wait_send()

    for block in range(wide.shape[1] // LANES):
        wide[:, block * LANES : (block + 1) * LANES] = out[
            block * size : (block + 1) * size, :
        ].astype(f32)


def kept_tokens(tok, first, clip_ref, flags_ref):
    token = lax.broadcasted_iota(jnp.int32, (8, tok), 1)
    kept = jnp.zeros((8, tok), jnp.int32)
    for block in range(tok // BLK):
        inside = (token >= block * BLK) & (token < (block + 1) * BLK)
        kept = jnp.where(inside, flags_ref[block], kept)
    before = token + first < clip_ref[0]
    return jnp.where(before & (kept == 1), 1.0, 0.0).astype(f32)[:1]


def step_kernel(
    chips, depth, pieces,
    q_hbm, k_hbm, v_hbm, qt_hbm, kt_hbm, vt_hbm, t_hbm, w_hbm, gain_ref, clip_ref, flags_ref,
    res_ref, gq_ref, grad_ref, k, v, valid_ref,
    q, qt, kt, vt, teach, weight, loads,
    wide1, near1, sent1, out1, half1, mine1, parts1,
    wide2, near2, sent2, out2, half2, mine2, parts2,
    unnorm, scale, normed, ngrad, ugrad, turned, gain,
    *sems,
):
    at = Where(chips, depth)
    tok = q.shape[1]
    incoming = [
        pltpu.make_async_copy(src, dst, loads.at[i])
        for i, (src, dst) in enumerate(
            [
                (k_hbm, k),
                (v_hbm, v),
                (kt_hbm, kt),
                (vt_hbm, vt),
                (w_hbm, weight),
                (q_hbm, q),
                (qt_hbm, qt),
                (t_hbm, teach),
            ]
        )
    ]
    greet(at)
    for load in incoming[:4]:
        load.start()

    device = lax.axis_index("seq") * depth + at.sub
    valid = kept_tokens(tok, device * tok, clip_ref, flags_ref)
    valid_ref[...] = jnp.broadcast_to(valid, valid_ref.shape)

    def head(ref, h):
        return ref[h * E : (h + 1) * E, :]

    def square(ref, h):
        return ref[:, h * E : (h + 1) * E].astype(bf16)

    def key_parts(h):
        keys = head(k, h).astype(f32)
        slope = jnp.where(keys > 0, 1.0, 0.0) * valid
        return jnp.maximum(keys, 0.0) * valid, slope

    edge = wide1.shape[1] - LANES
    wide1[:, edge:] = jnp.zeros((wide1.shape[0], LANES), f32)
    wide2[:, edge:] = jnp.zeros((wide2.shape[0], LANES), f32)
    for load in incoming[:4]:
        load.wait()
    for load in incoming[4:]:
        load.start()
    for h in range(H):
        feat, slope = key_parts(h)
        feat = feat.astype(bf16)
        along = (slope * head(kt, h).astype(f32)).astype(bf16)
        vals = head(v, h)
        cols = slice(h * E, (h + 1) * E)
        wide1[:E, cols] = dot(vals, feat, (1, 1))
        wide1[E:, cols] = dot(vals, along, (1, 1)) + dot(head(vt, h), feat, (1, 1))

    def prepare():
        row = lax.broadcasted_iota(jnp.int32, (E, E), 0)
        col = lax.broadcasted_iota(jnp.int32, (E, E), 1)
        for h in range(H):
            spread = jnp.where(row == col, gain_ref[h * E : (h + 1) * E][None, :], 0.0)
            gain[h * E : (h + 1) * E, :] = jnp.sum(spread, axis=1, keepdims=True)
        for load in incoming[4:]:
            load.wait()
        for start in range(0, weight.shape[1], 256):
            stop = min(start + 256, weight.shape[1])
            turned[start:stop, :] = weight[:, start:stop].T

    pl.semaphore_wait(pltpu.get_barrier_semaphore(), chips)
    all_total(
        at, pieces[0], wide1, near1, sent1, out1, half1, mine1, parts1, sems[:8], None, prepare
    )

    def query(h):
        rows = head(q, h).astype(f32)
        return jnp.maximum(rows, 0.0).astype(bf16), jnp.where(rows > 0, 1.0, 0.0).astype(f32)

    for h in range(H):
        rows = slice(h * E, (h + 1) * E)
        both = square(wide1, h)
        feat, slope = query(h)
        along = (slope * head(qt, h).astype(f32)).astype(bf16)
        un = dot(both[:E], feat, (1, 0))
        un_dot = dot(both[:E], along, (1, 0)) + dot(both[E:], feat, (1, 0))
        inv = lax.rsqrt(jnp.mean(un * un, axis=0, keepdims=True) + 1e-06)
        unnorm[rows, :] = un
        scale[h] = inv
        normed[rows, :] = (gain[rows, :] * norm_back(un, inv, un_dot)).astype(bf16)

    velocity = dot(turned[...], normed[...], (1, 0))
    res_ref[...] = (velocity - teach[...].astype(f32)).astype(bf16)
    ngrad[...] = dot(weight[...], res_ref[...], (1, 0))
    for h in range(H):
        rows = slice(h * E, (h + 1) * E)
        weighted = gain[rows, :] * head(ngrad, h)
        grad = norm_back(head(unnorm, h), scale[h], weighted).astype(bf16)
        ugrad[rows, :] = grad
        wide2[:, h * E : (h + 1) * E] = dot(grad, query(h)[0], (1, 1))

    def query_grads():
        for h in range(H):
            back = dot(square(wide1, h)[:E], head(ugrad, h), (0, 0))
            gq_ref[h * E : (h + 1) * E, :] = (query(h)[1] * back).astype(bf16)

    all_total(
        at, pieces[1], wide2, near2, sent2, out2, half2, mine2, parts2, sems[8:], None, query_grads
    )

    grad_ref[...] = wide2[...].astype(bf16)


def finish_kernel(
    k, v, res, gq, grad_ref, valid_ref,
    res_out, gq_out, gk_out, gv_out,
    gk, gv, stores,
):
    whole = [
        pltpu.make_async_copy(src, dst, stores.at[2 * H + i])
        for i, (src, dst) in enumerate([(res, res_out), (gq, gq_out)])
    ]
    for store in whole:
        store.start()
    valid = valid_ref[:1, :]
    outgoing = []
    for h in range(H):
        rows = slice(h * E, (h + 1) * E)
        total = grad_ref[:, rows]
        keys = k[rows, :].astype(f32)
        slope = jnp.where(keys > 0, 1.0, 0.0) * valid
        feat = (jnp.maximum(keys, 0.0) * valid).astype(bf16)
        gk[rows, :] = (slope * dot(total, v[rows, :], (0, 0))).astype(bf16)
        gv[rows, :] = dot(total, feat, (1, 0)).astype(bf16)
        for i, (src, dst) in enumerate([(gk, gk_out), (gv, gv_out)]):
            outgoing.append(
                pltpu.make_async_copy(src.at[rows], dst.at[rows], stores.at[2 * h + i])
            )
            outgoing[-1].start()
    for store in whole + outgoing:
        store.wait()


def local(
    query_rows,
    key_rows,
    value_rows,
    query_tangent,
    key_tangent,
    value_tangent,
    teacher,
    out_weight,
    norm_gain,
    clip_length,
    block_mask,
):
    tok, width = query_rows.shape
    depth = lax.axis_size("sub")
    chips = lax.axis_size("seq") // 2 * depth
    padded = -(-width // LANES) * LANES
    vmem = pltpu.VMEM
    dma = pltpu.SemaphoreType.DMA
    pieces = []
    totals = []
    for size in (2 * E, E):
        piece = -(-(size * padded // LANES) // (32 * chips)) * 16
        pieces.append(piece)
        half = (chips * piece, LANES)
        full = (2 * chips * piece, LANES)
        totals += [vmem((size, padded), f32), vmem(full, f32), vmem(full, bf16), vmem(full, bf16)]
        totals += [vmem(half, bf16)] * 3
    arrays = (query_rows, key_rows, value_rows, query_tangent, key_tangent, value_tangent)
    arrays = tuple(array.T for array in arrays + (teacher,)) + (out_weight,)
    anywhere = pl.BlockSpec(memory_space=pltpu.HBM)
    in_vmem = pl.BlockSpec(memory_space=vmem)
    in_smem = pl.BlockSpec(memory_space=pltpu.SMEM)
    wide_t = jax.ShapeDtypeStruct((width, tok), bf16)
    res_t = jax.ShapeDtypeStruct(teacher.shape[::-1], bf16)
    handed = [(res_t.shape, bf16), (wide_t.shape, bf16), ((E, padded), bf16)]
    handed += [(wide_t.shape, bf16)] * 2 + [((8, tok), f32)]
    held = sum(rows * cols * jnp.dtype(kind).itemsize for (rows, cols), kind in handed)
    res, grad_query, grad, keys, values, valid = pl.pallas_call(
        functools.partial(step_kernel, chips, depth, pieces),
        out_shape=[vmem(*piece) for piece in handed],
        in_specs=[anywhere] * 8 + [in_vmem, in_smem, in_smem],
        out_specs=[in_vmem] * 6,
        scratch_shapes=[vmem(arrays[i].shape, bf16) for i in (0, 3, 4, 5, 6, 7)]
        + [dma((8,))]
        + totals
        + [
            vmem((width, tok), f32),
            vmem((H, 1, tok), f32),
            vmem((width, tok), bf16),
            vmem((width, tok), f32),
            vmem((width, tok), bf16),
            vmem(out_weight.shape[::-1], bf16),
            vmem((width, 1), f32),
        ]
        + ([dma, dma] + [dma((chips,))] * 6) * 2,
        compiler_params=pltpu.CompilerParams(
            collective_id=0, has_side_effects=True, vmem_limit_bytes=VMEM_BYTES - held
        ),
    )(*arrays, norm_gain, clip_length, block_mask)
    outs = pl.pallas_call(
        finish_kernel,
        out_shape=(res_t, wide_t, wide_t, wide_t),
        in_specs=[in_vmem] * 6,
        out_specs=[anywhere] * 4,
        scratch_shapes=[vmem(wide_t.shape, bf16)] * 2 + [dma((2 * H + 2,))],
        compiler_params=pltpu.CompilerParams(vmem_limit_bytes=FINISH_VMEM),
    )(keys, values, res, grad_query, grad, valid)
    return tuple(out.T for out in outs)


def solution(mesh):
    return jax.shard_map(
        local,
        mesh=mesh,
        in_specs=(
            P(("seq", "sub"), None),
            P(("seq", "sub"), None),
            P(("seq", "sub"), None),
            P(("seq", "sub"), None),
            P(("seq", "sub"), None),
            P(("seq", "sub"), None),
            P(("seq", "sub"), None),
            P(),
            P(),
            P(),
            P(("seq", "sub")),
        ),
        out_specs=(
            P(("seq", "sub"), None),
            P(("seq", "sub"), None),
            P(("seq", "sub"), None),
            P(("seq", "sub"), None),
        ),
        check_vma=False,
    )
```

```python
import functools

import jax
import jax.numpy as jnp
from jax import lax
from jax.experimental import pallas as pl
from jax.experimental.pallas import tpu as pltpu
from jax.sharding import PartitionSpec as P

H = 10
E = 112
BLK = 64


MESH = pl.DeviceIdType.MESH
LANES = 128
VMEM_BYTES = 67043328
FINISH_VMEM = 16 << 20
f32 = jnp.float32
bf16 = jnp.bfloat16


def norm_back(unnorm, scale_inv, weighted):
    inner_mean = jnp.mean(unnorm * weighted, axis=0, keepdims=True)
    return scale_inv * weighted - unnorm * (scale_inv * scale_inv * scale_inv) * inner_mean


def dot(left, right, over):
    return lax.dot_general(left, right, ((over[:1], over[1:]), ((), ())), preferred_element_type=f32)


class Where:
    def __init__(self, chips, depth):
        seq = lax.axis_index("seq")
        self.sub = lax.axis_index("sub")
        self.depth = depth
        self.planes = chips // depth
        self.layers = depth // 2
        self.group = chips // 2
        self.core = lax.rem(seq, 2)
        self.column = seq // 2
        self.layer = lax.rem(self.sub, self.layers)
        self.spot = self.column * self.layers + self.layer
        self.partner = (seq + 1 - 2 * self.core, self.sub)
        self.opposite = (self.partner[0], lax.rem(self.sub + self.layers, depth))

    def peer(self, spot):
        base = self.sub - self.layer
        seq = (spot // self.layers) * 2 + 1 - self.core
        return seq, base + lax.rem(spot, self.layers)

    def each(self, body, near_first=False):
        levels = range(self.layers) if near_first else range(self.layers)[::-1]
        for level in levels:
            layer = lax.rem(self.layer + level, self.layers)

            @pl.loop(0 if level else 1, self.planes)
            def _(step):
                body(lax.rem(self.column + step, self.planes) * self.layers + layer)


def greet(at):
    barrier = pltpu.get_barrier_semaphore()

    def hello(device):
        pl.semaphore_signal(barrier, inc=1, device_id=device, device_id_type=MESH)

    hello(at.opposite)
    at.each(lambda spot: hello(at.peer(spot)))
    hello(at.partner)


class Total:
    def __init__(self, at, piece, wide, near, sent, out, half, mine, parts, cross, sems):
        self.at, self.piece, self.wide = at, piece, wide
        self.near, self.sent, self.out = near, sent, out
        self.half, self.mine, self.parts, self.cross, self.sems = half, mine, parts, cross, sems

    def copy(self, src, dst, send, recv, to):
        return pltpu.make_async_remote_copy(
            src_ref=src,
            dst_ref=dst,
            send_sem=send,
            recv_sem=recv,
            device_id=to,
            device_id_type=MESH,
        )

    def rows(self, spot, side=None):
        base = spot if side is None else side * self.at.group + spot
        return pl.ds(pl.multiple_of(base * self.piece, 16), self.piece)

    def swap(self):
        span = self.at.group * self.piece
        other = pl.ds(pl.multiple_of((1 - self.at.core) * span, 16), span)
        return self.copy(
            self.sent.at[other], self.half, self.sems[0], self.sems[1], self.at.partner
        )

    def scatter(self, spot, slot):
        return self.copy(
            self.mine.at[self.rows(spot)],
            self.parts.at[self.rows(slot)],
            self.sems[2].at[spot],
            self.sems[3].at[slot],
            self.at.peer(spot),
        )

    def exchange(self):
        return [
            self.copy(
                self.cross.at[2],
                self.cross.at[i],
                self.sems[4].at[i],
                self.sems[5].at[i],
                to,
            )
            for i, to in enumerate([self.at.partner, self.at.opposite])
        ]

    def gather(self, spot, slot, side):
        return self.copy(
            self.out.at[self.rows(slot, side)],
            self.out.at[self.rows(slot, side)],
            self.sems[6].at[spot],
            self.sems[7].at[slot],
            self.at.peer(spot),
        )

    def forward(self, spot, side):
        return self.copy(
            self.out.at[self.rows(spot, side)],
            self.out.at[self.rows(spot, side)],
            self.sems[8].at[spot],
            self.sems[9].at[spot],
            self.at.partner,
        )

    def clear_edge(self):
        edge = self.wide.shape[1] - LANES
        self.wide[:, edge:] = jnp.zeros((self.wide.shape[0], LANES), f32)

    def pack(self):
        size = self.wide.shape[0]
        blocks = self.wide.shape[1] // LANES
        for block in range(blocks):
            lanes = self.wide[:, block * LANES : (block + 1) * LANES]
            self.near[block * size : (block + 1) * size, :] = lanes
            self.sent[block * size : (block + 1) * size, :] = lanes.astype(bf16)
        used = size * blocks
        left = self.near.shape[0] - used
        if left:
            self.near[used:, :] = jnp.zeros((left, LANES), f32)
            self.sent[used:, :] = jnp.zeros((left, LANES), bf16)

    def spread(self):
        at = self.at

        def one(spot):
            own = self.near[self.rows(spot, at.core), :]
            both = own + self.half[self.rows(spot), :].astype(f32)
            self.mine[self.rows(spot), :] = both.astype(bf16)
            self.scatter(spot, at.spot).start()

        at.each(one)
        one(at.spot)

    def reduce(self):
        at = self.at

        def add(spot):
            self.scatter(spot, spot).wait_recv()
            self.near[: self.piece, :] += self.parts[self.rows(spot), :].astype(f32)

        self.scatter(at.spot, at.spot).wait_recv()
        self.near[: self.piece, :] = self.parts[self.rows(at.spot), :].astype(f32)
        at.each(add, near_first=True)
        self.cross[2] = self.near[: self.piece, :].astype(bf16)
        for copy in self.exchange()[::-1]:
            copy.start()

    def settle(self):
        at = self.at
        for copy in self.exchange():
            copy.wait_recv()
        both = self.cross[0].astype(f32) + self.cross[1].astype(f32)
        self.out[self.rows(at.spot, at.core), :] = both.astype(bf16)

        def one(spot):
            self.gather(spot, at.spot, at.core).start()

        at.each(one)
        one(at.spot)

    def relay(self):
        side = 1 - self.at.core

        def one(spot):
            self.gather(spot, spot, side).wait_recv()
            self.forward(spot, side).start()

        self.at.each(one, near_first=True)
        self.gather(self.at.spot, self.at.spot, side).wait_recv()

    def arrive(self):
        at = self.at
        at.each(lambda spot: self.forward(spot, at.core).wait_recv(), near_first=True)
        size = self.wide.shape[0]
        for block in range(self.wide.shape[1] // LANES):
            self.wide[:, block * LANES : (block + 1) * LANES] = self.out[
                block * size : (block + 1) * size, :
            ].astype(f32)

    def drain(self):
        at = self.at
        self.swap().wait_send()

        def one(spot):
            self.scatter(spot, at.spot).wait_send()
            self.gather(spot, at.spot, at.core).wait_send()

        def other(spot):
            one(spot)
            self.forward(spot, 1 - at.core).wait_send()

        at.each(other)
        one(at.spot)
        for copy in self.exchange():
            copy.wait_send()


def kept_tokens(tok, first, clip_ref, flags_ref):
    token = lax.broadcasted_iota(jnp.int32, (8, tok), 1)
    kept = jnp.zeros((8, tok), jnp.int32)
    for block in range(tok // BLK):
        inside = (token >= block * BLK) & (token < (block + 1) * BLK)
        kept = jnp.where(inside, flags_ref[block], kept)
    before = token + first < clip_ref[0]
    return jnp.where(before & (kept == 1), 1.0, 0.0).astype(f32)[:1]


def step_kernel(
    chips, depth, piece,
    q_hbm, k_hbm, v_hbm, qt_hbm, kt_hbm, vt_hbm, t_hbm, w_hbm, gain_hbm, clip_hbm, flags_hbm,
    res_ref, gq_ref, grad_ref, k, v, valid_ref,
    q, qt, kt, vt, teach, weight, gain_ref, clip_ref, flags_ref, loads,
    states, part, unnorm, scale, normed, ngrad, ugrad, turned, gain,
    *rest,
):
    at = Where(chips, depth)
    greet(at)
    tok = q.shape[1]
    pairs = [
        (k_hbm, k),
        (v_hbm, v),
        (clip_hbm, clip_ref),
        (flags_hbm, flags_ref),
        (kt_hbm, kt),
        (vt_hbm, vt),
        (w_hbm, weight),
        (q_hbm, q),
        (qt_hbm, qt),
        (gain_hbm, gain_ref),
        (t_hbm, teach),
    ]
    incoming = [pltpu.make_async_copy(*pair, loads.at[i]) for i, pair in enumerate(pairs)]
    for load in incoming[:6]:
        load.start()
    state, state_dot, state_grad = (
        Total(at, piece, *rest[8 * i : 8 * i + 8], rest[24 + 10 * i : 34 + 10 * i]) for i in range(3)
    )

    def head(ref, h):
        return ref[h * E : (h + 1) * E, :]

    def square(ref, h):
        return ref[:, h * E : (h + 1) * E].astype(bf16)

    def cols(h):
        return slice(h * E, (h + 1) * E)

    for total in (state, state_dot, state_grad):
        total.clear_edge()
    for load in incoming[:4]:
        load.wait()
    for load in incoming[6:]:
        load.start()
    device = lax.axis_index("seq") * depth + at.sub
    valid = kept_tokens(tok, device * tok, clip_ref, flags_ref)
    valid_ref[...] = jnp.broadcast_to(valid, valid_ref.shape)
    for h in range(H):
        feat = (jnp.maximum(head(k, h).astype(f32), 0.0) * valid).astype(bf16)
        ugrad[cols(h), :] = feat
        state.wide[:, cols(h)] = dot(head(v, h), feat, (1, 1))
    state.pack()
    pl.semaphore_wait(pltpu.get_barrier_semaphore(), at.group + 1)
    state.swap().start()
    for load in incoming[4:6]:
        load.wait()
    for h in range(H):
        slope = jnp.where(head(k, h).astype(f32) > 0, 1.0, 0.0) * valid
        along = (slope * head(kt, h).astype(f32)).astype(bf16)
        state_dot.wide[:, cols(h)] = dot(head(v, h), along, (1, 1)) + dot(
            head(vt, h), head(ugrad, h), (1, 1)
        )
    state_dot.pack()
    state_dot.swap().start()
    state.swap().wait_recv()
    state.spread()
    state_dot.swap().wait_recv()
    state_dot.spread()

    for load in incoming[6:]:
        load.wait()
    row = lax.broadcasted_iota(jnp.int32, (E, E), 0)
    col = lax.broadcasted_iota(jnp.int32, (E, E), 1)
    for h in range(H):
        spread = jnp.where(row == col, gain_ref[cols(h)][None, :], 0.0)
        gain[cols(h), :] = jnp.sum(spread, axis=1, keepdims=True)
    for start in range(0, weight.shape[1], 256):
        stop = min(start + 256, weight.shape[1])
        turned[start:stop, :] = weight[:, start:stop].T

    state.reduce()
    state_dot.reduce()
    state.settle()
    state_dot.settle()

    def query(h):
        rows = head(q, h).astype(f32)
        return jnp.maximum(rows, 0.0).astype(bf16), jnp.where(rows > 0, 1.0, 0.0).astype(f32)

    state.relay()
    state.arrive()
    for h in range(H):
        feat, slope = query(h)
        along = (slope * head(qt, h).astype(f32)).astype(bf16)
        matrix = square(state.wide, h)
        states[h] = matrix
        un = dot(matrix, feat, (1, 0))
        unnorm[cols(h), :] = un
        scale[h] = lax.rsqrt(jnp.mean(un * un, axis=0, keepdims=True) + 1e-06)
        part[cols(h), :] = dot(matrix, along, (1, 0))
    state_dot.relay()
    state_dot.arrive()
    for h in range(H):
        un_dot = head(part, h) + dot(square(state_dot.wide, h), query(h)[0], (1, 0))
        back = norm_back(head(unnorm, h), scale[h], un_dot)
        normed[cols(h), :] = (gain[cols(h), :] * back).astype(bf16)

    velocity = dot(turned[...], normed[...], (1, 0))
    res_ref[...] = (velocity - teach[...].astype(f32)).astype(bf16)
    ngrad[...] = dot(weight[...], res_ref[...], (1, 0))
    for h in range(H):
        weighted = gain[cols(h), :] * head(ngrad, h)
        grad = norm_back(head(unnorm, h), scale[h], weighted).astype(bf16)
        ugrad[cols(h), :] = grad
        state_grad.wide[:, cols(h)] = dot(grad, query(h)[0], (1, 1))
    state_grad.pack()
    state_grad.swap().start()
    state_grad.swap().wait_recv()
    state_grad.spread()
    for h in range(H):
        back = dot(states[h], head(ugrad, h), (0, 0))
        gq_ref[cols(h), :] = (query(h)[1] * back).astype(bf16)
    state.drain()
    state_dot.drain()
    state_grad.reduce()
    state_grad.settle()
    state_grad.relay()
    state_grad.arrive()
    grad_ref[...] = state_grad.wide[...].astype(bf16)
    state_grad.drain()


def finish_kernel(
    k, v, res, gq, grad_ref, valid_ref,
    res_out, gq_out, gk_out, gv_out,
    gk, gv, stores,
):
    whole = [
        pltpu.make_async_copy(src, dst, stores.at[2 * H + i])
        for i, (src, dst) in enumerate([(res, res_out), (gq, gq_out)])
    ]
    for store in whole:
        store.start()
    valid = valid_ref[:1, :]
    outgoing = []
    for h in range(H):
        rows = slice(h * E, (h + 1) * E)
        total = grad_ref[:, rows]
        keys = k[rows, :].astype(f32)
        slope = jnp.where(keys > 0, 1.0, 0.0) * valid
        feat = (jnp.maximum(keys, 0.0) * valid).astype(bf16)
        gk[rows, :] = (slope * dot(total, v[rows, :], (0, 0))).astype(bf16)
        gv[rows, :] = dot(total, feat, (1, 0)).astype(bf16)
        for i, (src, dst) in enumerate([(gk, gk_out), (gv, gv_out)]):
            outgoing.append(
                pltpu.make_async_copy(src.at[rows], dst.at[rows], stores.at[2 * h + i])
            )
            outgoing[-1].start()
    for store in whole + outgoing:
        store.wait()


def local(
    query_rows,
    key_rows,
    value_rows,
    query_tangent,
    key_tangent,
    value_tangent,
    teacher,
    out_weight,
    norm_gain,
    clip_length,
    block_mask,
):
    tok, width = query_rows.shape
    depth = lax.axis_size("sub")
    chips = lax.axis_size("seq") // 2 * depth
    padded = -(-width // LANES) * LANES
    vmem = pltpu.VMEM
    dma = pltpu.SemaphoreType.DMA
    group = chips // 2
    piece = -(-(E * padded // LANES) // (32 * group)) * 16
    half = (group * piece, LANES)
    full = (2 * group * piece, LANES)
    total = [vmem((E, padded), f32), vmem(full, f32), vmem(full, bf16), vmem(full, bf16)]
    total += [vmem(half, bf16)] * 3 + [vmem((3, piece, LANES), bf16)]
    arrays = (query_rows, key_rows, value_rows, query_tangent, key_tangent, value_tangent)
    arrays = tuple(array.T for array in arrays + (teacher,)) + (out_weight,)
    anywhere = pl.BlockSpec(memory_space=pltpu.HBM)
    in_vmem = pl.BlockSpec(memory_space=vmem)
    wide_t = jax.ShapeDtypeStruct((width, tok), bf16)
    res_t = jax.ShapeDtypeStruct(teacher.shape[::-1], bf16)
    handed = [(res_t.shape, bf16), (wide_t.shape, bf16), ((E, padded), bf16)]
    handed += [(wide_t.shape, bf16)] * 2 + [((8, tok), f32)]
    held = sum(rows * cols * jnp.dtype(kind).itemsize for (rows, cols), kind in handed)
    res, grad_query, grad, keys, values, valid = pl.pallas_call(
        functools.partial(step_kernel, chips, depth, piece),
        out_shape=[vmem(*piece) for piece in handed],
        in_specs=[anywhere] * 11,
        out_specs=[in_vmem] * 6,
        scratch_shapes=[vmem(arrays[i].shape, bf16) for i in (0, 3, 4, 5, 6, 7)]
        + [vmem(norm_gain.shape, f32)]
        + [pltpu.SMEM(array.shape, jnp.int32) for array in (clip_length, block_mask)]
        + [dma((11,))]
        + [
            vmem((H, E, E), bf16),
            vmem((width, tok), f32),
            vmem((width, tok), f32),
            vmem((H, 1, tok), f32),
            vmem((width, tok), bf16),
            vmem((width, tok), f32),
            vmem((width, tok), bf16),
            vmem(out_weight.shape[::-1], bf16),
            vmem((width, 1), f32),
        ]
        + total * 3
        + ([dma, dma] + [dma((group,))] * 2 + [dma((2,))] * 2 + [dma((group,))] * 4) * 3,
        compiler_params=pltpu.CompilerParams(
            collective_id=0, has_side_effects=True, vmem_limit_bytes=VMEM_BYTES - held
        ),
    )(*arrays, norm_gain, clip_length, block_mask)
    outs = pl.pallas_call(
        finish_kernel,
        out_shape=(res_t, wide_t, wide_t, wide_t),
        in_specs=[in_vmem] * 6,
        out_specs=[anywhere] * 4,
        scratch_shapes=[vmem(wide_t.shape, bf16)] * 2 + [dma((2 * H + 2,))],
        compiler_params=pltpu.CompilerParams(vmem_limit_bytes=FINISH_VMEM),
    )(keys, values, res, grad_query, grad, valid)
    return tuple(out.T for out in outs)


def solution(mesh):
    return jax.shard_map(
        local,
        mesh=mesh,
        in_specs=(
            P(("seq", "sub"), None),
            P(("seq", "sub"), None),
            P(("seq", "sub"), None),
            P(("seq", "sub"), None),
            P(("seq", "sub"), None),
            P(("seq", "sub"), None),
            P(("seq", "sub"), None),
            P(),
            P(),
            P(),
            P(("seq", "sub")),
        ),
        out_specs=(
            P(("seq", "sub"), None),
            P(("seq", "sub"), None),
            P(("seq", "sub"), None),
            P(("seq", "sub"), None),
        ),
        check_vma=False,
    )
```

```python
import functools

import jax
import jax.numpy as jnp
from jax import lax
from jax.experimental import pallas as pl
from jax.experimental.pallas import tpu as pltpu
from jax.sharding import PartitionSpec as P

H = 10
E = 112
BLK = 64


MESH = pl.DeviceIdType.MESH
LANES = 128
VMEM_BYTES = 67043328
FINISH_VMEM = 16 << 20
f32 = jnp.float32
bf16 = jnp.bfloat16


def norm_back(unnorm, scale_inv, weighted):
    inner_mean = jnp.mean(unnorm * weighted, axis=0, keepdims=True)
    return scale_inv * weighted - unnorm * (scale_inv * scale_inv * scale_inv) * inner_mean


def dot(left, right, over):
    return lax.dot_general(left, right, ((over[:1], over[1:]), ((), ())), preferred_element_type=f32)


class Where:
    def __init__(self, chips, depth):
        seq = lax.axis_index("seq")
        self.sub = lax.axis_index("sub")
        self.depth = depth
        self.planes = chips // depth
        self.layers = depth // 2
        self.group = chips // 2
        self.core = lax.rem(seq, 2)
        self.column = seq // 2
        self.layer = lax.rem(self.sub, self.layers)
        self.spot = self.column * self.layers + self.layer
        self.partner = (seq + 1 - 2 * self.core, self.sub)
        self.opposite = (self.partner[0], lax.rem(self.sub + self.layers, depth))

    def peer(self, spot):
        base = self.sub - self.layer
        seq = (spot // self.layers) * 2 + 1 - self.core
        return seq, base + lax.rem(spot, self.layers)

    def each(self, body, near_first=False):
        levels = range(self.layers) if near_first else range(self.layers)[::-1]
        for level in levels:
            layer = lax.rem(self.layer + level, self.layers)

            @pl.loop(0 if level else 1, self.planes)
            def _(step):
                body(lax.rem(self.column + step, self.planes) * self.layers + layer)


def greet(at):
    barrier = pltpu.get_barrier_semaphore()

    def hello(device):
        pl.semaphore_signal(barrier, inc=1, device_id=device, device_id_type=MESH)

    hello(at.opposite)
    at.each(lambda spot: hello(at.peer(spot)))
    hello(at.partner)


class Total:
    def __init__(self, at, blocks, wide, near, sent, out, half, mine, parts, cross, sems):
        self.at, self.blocks, self.wide = at, blocks, wide
        self.piece = cross.shape[1]
        self.near, self.sent, self.out = near, sent, out
        self.half, self.mine, self.parts, self.cross, self.sems = half, mine, parts, cross, sems

    def copy(self, src, dst, send, recv, to):
        return pltpu.make_async_remote_copy(
            src_ref=src,
            dst_ref=dst,
            send_sem=send,
            recv_sem=recv,
            device_id=to,
            device_id_type=MESH,
        )

    def rows(self, spot, side=None):
        base = spot if side is None else side * self.at.group + spot
        return pl.ds(pl.multiple_of(base * self.piece, 16), self.piece)

    def swap(self):
        span = self.at.group * self.piece
        other = pl.ds(pl.multiple_of((1 - self.at.core) * span, 16), span)
        return self.copy(
            self.sent.at[other], self.half, self.sems[0], self.sems[1], self.at.partner
        )

    def scatter(self, spot, slot):
        return self.copy(
            self.mine.at[self.rows(spot)],
            self.parts.at[self.rows(slot)],
            self.sems[2].at[spot],
            self.sems[3].at[slot],
            self.at.peer(spot),
        )

    def exchange(self):
        return [
            self.copy(
                self.cross.at[2],
                self.cross.at[i],
                self.sems[4].at[i],
                self.sems[5].at[i],
                to,
            )
            for i, to in enumerate([self.at.partner, self.at.opposite])
        ]

    def gather(self, spot, slot, side):
        return self.copy(
            self.out.at[self.rows(slot, side)],
            self.out.at[self.rows(slot, side)],
            self.sems[6].at[spot],
            self.sems[7].at[slot],
            self.at.peer(spot),
        )

    def forward(self, spot, side):
        return self.copy(
            self.out.at[self.rows(spot, side)],
            self.out.at[self.rows(spot, side)],
            self.sems[8].at[spot],
            self.sems[9].at[spot],
            self.at.partner,
        )

    def views(self):
        size = self.wide.shape[0]
        for step, block in enumerate(self.blocks):
            yield (
                slice(block * LANES, (block + 1) * LANES),
                slice(step * size, (step + 1) * size),
            )

    def pack(self):
        for cols, rows in self.views():
            lanes = self.wide[:, cols]
            self.near[rows, :] = lanes
            self.sent[rows, :] = lanes.astype(bf16)
        used = self.wide.shape[0] * len(self.blocks)
        left = self.near.shape[0] - used
        if left:
            self.near[used:, :] = jnp.zeros((left, LANES), f32)
            self.sent[used:, :] = jnp.zeros((left, LANES), bf16)

    def spread(self):
        at = self.at

        def one(spot):
            own = self.near[self.rows(spot, at.core), :]
            both = own + self.half[self.rows(spot), :].astype(f32)
            self.mine[self.rows(spot), :] = both.astype(bf16)
            self.scatter(spot, at.spot).start()

        at.each(one)
        one(at.spot)

    def reduce(self):
        at = self.at

        def add(spot):
            self.scatter(spot, spot).wait_recv()
            self.near[: self.piece, :] += self.parts[self.rows(spot), :].astype(f32)

        self.scatter(at.spot, at.spot).wait_recv()
        self.near[: self.piece, :] = self.parts[self.rows(at.spot), :].astype(f32)
        at.each(add, near_first=True)
        self.cross[2] = self.near[: self.piece, :].astype(bf16)
        for copy in self.exchange()[::-1]:
            copy.start()

    def settle(self):
        at = self.at
        for copy in self.exchange():
            copy.wait_recv()
        both = self.cross[0].astype(f32) + self.cross[1].astype(f32)
        self.out[self.rows(at.spot, at.core), :] = both.astype(bf16)

        def one(spot):
            self.gather(spot, at.spot, at.core).start()

        at.each(one)
        one(at.spot)

    def relay(self):
        side = 1 - self.at.core

        def one(spot):
            self.gather(spot, spot, side).wait_recv()
            self.forward(spot, side).start()

        self.at.each(one, near_first=True)
        self.gather(self.at.spot, self.at.spot, side).wait_recv()

    def arrive(self, result):
        at = self.at
        at.each(lambda spot: self.forward(spot, at.core).wait_recv(), near_first=True)
        for cols, rows in self.views():
            result[:, cols] = self.out[rows, :].astype(result.dtype)

    def drain(self):
        at = self.at
        self.swap().wait_send()

        def one(spot):
            self.scatter(spot, at.spot).wait_send()
            self.gather(spot, at.spot, at.core).wait_send()

        def other(spot):
            one(spot)
            self.forward(spot, 1 - at.core).wait_send()

        at.each(other)
        one(at.spot)
        for copy in self.exchange():
            copy.wait_send()


def kept_tokens(tok, first, clip_ref, flags_ref):
    token = lax.broadcasted_iota(jnp.int32, (8, tok), 1)
    kept = jnp.zeros((8, tok), jnp.int32)
    for block in range(tok // BLK):
        inside = (token >= block * BLK) & (token < (block + 1) * BLK)
        kept = jnp.where(inside, flags_ref[block], kept)
    before = token + first < clip_ref[0]
    return jnp.where(before & (kept == 1), 1.0, 0.0).astype(f32)[:1]


def step_kernel(
    chips, depth, spans,
    q_hbm, k_hbm, v_hbm, qt_hbm, kt_hbm, vt_hbm, t_hbm, w_hbm, gain_hbm, clip_hbm, flags_hbm,
    res_ref, gq_ref, grad_ref, k, v, valid_ref,
    q, qt, kt, vt, teach, weight, gain_ref, clip_ref, flags_ref, loads,
    states, part, unnorm, scale, normed, ngrad, ugrad, turned, gain,
    *rest,
):
    at = Where(chips, depth)
    greet(at)
    tok = q.shape[1]
    pairs = [
        (k_hbm, k),
        (v_hbm, v),
        (clip_hbm, clip_ref),
        (flags_hbm, flags_ref),
        (kt_hbm, kt),
        (vt_hbm, vt),
        (w_hbm, weight),
        (q_hbm, q),
        (qt_hbm, qt),
        (gain_hbm, gain_ref),
        (t_hbm, teach),
    ]
    incoming = [pltpu.make_async_copy(*pair, loads.at[i]) for i, pair in enumerate(pairs)]
    for load in incoming[:6]:
        load.start()
    wides = rest[:3]
    bufs, sems = rest[3 : 3 + 7 * len(spans)], rest[3 + 7 * len(spans) :]
    state, state_dot, early, late = (
        Total(
            at, span, wides[min(i, 2)], *bufs[7 * i : 7 * i + 7], sems[10 * i : 10 * i + 10]
        )
        for i, span in enumerate(spans)
    )
    lead = -(-len(early.blocks) * LANES // E)

    def head(ref, h):
        return ref[h * E : (h + 1) * E, :]

    def square(ref, h):
        return ref[:, h * E : (h + 1) * E].astype(bf16)

    def cols(h):
        return slice(h * E, (h + 1) * E)

    for wide in wides:
        edge = wide.shape[1] - LANES
        wide[:, edge:] = jnp.zeros((wide.shape[0], LANES), f32)
    for load in incoming[:4]:
        load.wait()
    for load in incoming[6:]:
        load.start()
    device = lax.axis_index("seq") * depth + at.sub
    valid = kept_tokens(tok, device * tok, clip_ref, flags_ref)
    valid_ref[...] = jnp.broadcast_to(valid, valid_ref.shape)
    for h in range(H):
        feat = (jnp.maximum(head(k, h).astype(f32), 0.0) * valid).astype(bf16)
        ugrad[cols(h), :] = feat
        state.wide[:, cols(h)] = dot(head(v, h), feat, (1, 1))
    state.pack()
    pl.semaphore_wait(pltpu.get_barrier_semaphore(), at.group + 1)
    state.swap().start()
    for load in incoming[4:6]:
        load.wait()
    for h in range(H):
        slope = jnp.where(head(k, h).astype(f32) > 0, 1.0, 0.0) * valid
        along = (slope * head(kt, h).astype(f32)).astype(bf16)
        state_dot.wide[:, cols(h)] = dot(head(v, h), along, (1, 1)) + dot(
            head(vt, h), head(ugrad, h), (1, 1)
        )
    state_dot.pack()
    state_dot.swap().start()
    state.swap().wait_recv()
    state.spread()
    state_dot.swap().wait_recv()
    state_dot.spread()

    for load in incoming[6:]:
        load.wait()
    row = lax.broadcasted_iota(jnp.int32, (E, E), 0)
    col = lax.broadcasted_iota(jnp.int32, (E, E), 1)
    for h in range(H):
        spread = jnp.where(row == col, gain_ref[cols(h)][None, :], 0.0)
        gain[cols(h), :] = jnp.sum(spread, axis=1, keepdims=True)
    for start in range(0, weight.shape[1], 256):
        stop = min(start + 256, weight.shape[1])
        turned[start:stop, :] = weight[:, start:stop].T

    state.reduce()
    state_dot.reduce()
    state.settle()
    state_dot.settle()

    def query(h):
        rows = head(q, h).astype(f32)
        return jnp.maximum(rows, 0.0).astype(bf16), jnp.where(rows > 0, 1.0, 0.0).astype(f32)

    state.relay()
    state_dot.relay()
    state.arrive(state.wide)
    for h in range(H):
        feat, slope = query(h)
        along = (slope * head(qt, h).astype(f32)).astype(bf16)
        matrix = square(state.wide, h)
        states[h] = matrix
        un = dot(matrix, feat, (1, 0))
        unnorm[cols(h), :] = un
        scale[h] = lax.rsqrt(jnp.mean(un * un, axis=0, keepdims=True) + 1e-06)
        part[cols(h), :] = dot(matrix, along, (1, 0))
    state_dot.arrive(state_dot.wide)
    for h in range(H):
        un_dot = head(part, h) + dot(square(state_dot.wide, h), query(h)[0], (1, 0))
        back = norm_back(head(unnorm, h), scale[h], un_dot)
        normed[cols(h), :] = (gain[cols(h), :] * back).astype(bf16)

    velocity = dot(turned[...], normed[...], (1, 0))
    res_ref[...] = (velocity - teach[...].astype(f32)).astype(bf16)

    def grads(first, last):
        rows = slice(first * E, last * E)
        ngrad[rows, :] = dot(weight[rows, :], res_ref[...], (1, 0))
        for h in range(first, last):
            weighted = gain[cols(h), :] * head(ngrad, h)
            grad = norm_back(head(unnorm, h), scale[h], weighted).astype(bf16)
            ugrad[cols(h), :] = grad
            early.wide[:, cols(h)] = dot(grad, query(h)[0], (1, 1))

    grads(0, lead)
    early.pack()
    early.swap().start()
    grads(lead, H)
    late.pack()
    late.swap().start()
    early.swap().wait_recv()
    early.spread()
    late.swap().wait_recv()
    late.spread()
    for h in range(H):
        back = dot(states[h], head(ugrad, h), (0, 0))
        gq_ref[cols(h), :] = (query(h)[1] * back).astype(bf16)
    state.drain()
    state_dot.drain()
    early.reduce()
    late.reduce()
    early.settle()
    late.settle()
    early.relay()
    late.relay()
    early.arrive(grad_ref)
    late.arrive(grad_ref)
    early.drain()
    late.drain()


def finish_kernel(
    k, v, res, gq, grad_ref, valid_ref,
    res_out, gq_out, gk_out, gv_out,
    gk, gv, stores,
):
    whole = [
        pltpu.make_async_copy(src, dst, stores.at[2 * H + i])
        for i, (src, dst) in enumerate([(res, res_out), (gq, gq_out)])
    ]
    for store in whole:
        store.start()
    valid = valid_ref[:1, :]
    outgoing = []
    for h in range(H):
        rows = slice(h * E, (h + 1) * E)
        total = grad_ref[:, rows]
        keys = k[rows, :].astype(f32)
        slope = jnp.where(keys > 0, 1.0, 0.0) * valid
        feat = (jnp.maximum(keys, 0.0) * valid).astype(bf16)
        gk[rows, :] = (slope * dot(total, v[rows, :], (0, 0))).astype(bf16)
        gv[rows, :] = dot(total, feat, (1, 0)).astype(bf16)
        for i, (src, dst) in enumerate([(gk, gk_out), (gv, gv_out)]):
            outgoing.append(
                pltpu.make_async_copy(src.at[rows], dst.at[rows], stores.at[2 * h + i])
            )
            outgoing[-1].start()
    for store in whole + outgoing:
        store.wait()


def local(
    query_rows,
    key_rows,
    value_rows,
    query_tangent,
    key_tangent,
    value_tangent,
    teacher,
    out_weight,
    norm_gain,
    clip_length,
    block_mask,
):
    tok, width = query_rows.shape
    depth = lax.axis_size("sub")
    chips = lax.axis_size("seq") // 2 * depth
    padded = -(-width // LANES) * LANES
    vmem = pltpu.VMEM
    dma = pltpu.SemaphoreType.DMA
    group = chips // 2
    group = chips // 2
    blocks = padded // LANES
    cut = -(-blocks // 2)
    spans = [range(blocks)] * 2 + [range(cut), range(cut, blocks)]
    totals = [vmem((E, padded), f32)] * 3
    for span in spans:
        piece = -(-(E * len(span)) // (32 * group)) * 16
        half = (group * piece, LANES)
        full = (2 * group * piece, LANES)
        totals += [vmem(full, f32), vmem(full, bf16), vmem(full, bf16)]
        totals += [vmem(half, bf16)] * 3 + [vmem((3, piece, LANES), bf16)]
    arrays = (query_rows, key_rows, value_rows, query_tangent, key_tangent, value_tangent)
    arrays = tuple(array.T for array in arrays + (teacher,)) + (out_weight,)
    anywhere = pl.BlockSpec(memory_space=pltpu.HBM)
    in_vmem = pl.BlockSpec(memory_space=vmem)
    wide_t = jax.ShapeDtypeStruct((width, tok), bf16)
    res_t = jax.ShapeDtypeStruct(teacher.shape[::-1], bf16)
    handed = [(res_t.shape, bf16), (wide_t.shape, bf16), ((E, padded), bf16)]
    handed += [(wide_t.shape, bf16)] * 2 + [((8, tok), f32)]
    held = sum(rows * cols * jnp.dtype(kind).itemsize for (rows, cols), kind in handed)
    res, grad_query, grad, keys, values, valid = pl.pallas_call(
        functools.partial(step_kernel, chips, depth, spans),
        out_shape=[vmem(*piece) for piece in handed],
        in_specs=[anywhere] * 11,
        out_specs=[in_vmem] * 6,
        scratch_shapes=[vmem(arrays[i].shape, bf16) for i in (0, 3, 4, 5, 6, 7)]
        + [vmem(norm_gain.shape, f32)]
        + [pltpu.SMEM(array.shape, jnp.int32) for array in (clip_length, block_mask)]
        + [dma((11,))]
        + [
            vmem((H, E, E), bf16),
            vmem((width, tok), f32),
            vmem((width, tok), f32),
            vmem((H, 1, tok), f32),
            vmem((width, tok), bf16),
            vmem((width, tok), f32),
            vmem((width, tok), bf16),
            vmem(out_weight.shape[::-1], bf16),
            vmem((width, 1), f32),
        ]
        + totals
        + ([dma, dma] + [dma((group,))] * 2 + [dma((2,))] * 2 + [dma((group,))] * 4) * len(spans),
        compiler_params=pltpu.CompilerParams(
            collective_id=0, has_side_effects=True, vmem_limit_bytes=VMEM_BYTES - held
        ),
    )(*arrays, norm_gain, clip_length, block_mask)
    outs = pl.pallas_call(
        finish_kernel,
        out_shape=(res_t, wide_t, wide_t, wide_t),
        in_specs=[in_vmem] * 6,
        out_specs=[anywhere] * 4,
        scratch_shapes=[vmem(wide_t.shape, bf16)] * 2 + [dma((2 * H + 2,))],
        compiler_params=pltpu.CompilerParams(vmem_limit_bytes=FINISH_VMEM),
    )(keys, values, res, grad_query, grad, valid)
    return tuple(out.T for out in outs)


def solution(mesh):
    return jax.shard_map(
        local,
        mesh=mesh,
        in_specs=(
            P(("seq", "sub"), None),
            P(("seq", "sub"), None),
            P(("seq", "sub"), None),
            P(("seq", "sub"), None),
            P(("seq", "sub"), None),
            P(("seq", "sub"), None),
            P(("seq", "sub"), None),
            P(),
            P(),
            P(),
            P(("seq", "sub")),
        ),
        out_specs=(
            P(("seq", "sub"), None),
            P(("seq", "sub"), None),
            P(("seq", "sub"), None),
            P(("seq", "sub"), None),
        ),
        check_vma=False,
    )
```

```python
import functools

import jax
import jax.numpy as jnp
from jax import lax
from jax.experimental import pallas as pl
from jax.experimental.pallas import tpu as pltpu
from jax.sharding import PartitionSpec as P

H = 10
E = 112
BLK = 64


MESH = pl.DeviceIdType.MESH
LANES = 128
VMEM_BYTES = 67043328
FINISH_VMEM = 16 << 20
f32 = jnp.float32
bf16 = jnp.bfloat16


def norm_back(unnorm, scale_inv, weighted):
    inner_mean = jnp.mean(unnorm * weighted, axis=0, keepdims=True)
    return scale_inv * weighted - unnorm * (scale_inv * scale_inv * scale_inv) * inner_mean


def dot(left, right, over):
    return lax.dot_general(left, right, ((over[:1], over[1:]), ((), ())), preferred_element_type=f32)


class Where:
    def __init__(self, chips, depth):
        seq = lax.axis_index("seq")
        self.sub = lax.axis_index("sub")
        self.depth = depth
        self.planes = chips // depth
        self.layers = depth // 2
        self.group = chips // 2
        self.core = lax.rem(seq, 2)
        self.column = seq // 2
        self.layer = lax.rem(self.sub, self.layers)
        self.spot = self.column * self.layers + self.layer
        self.partner = (seq + 1 - 2 * self.core, self.sub)
        self.opposite = (self.partner[0], lax.rem(self.sub + self.layers, depth))

    def peer(self, spot):
        base = self.sub - self.layer
        seq = (spot // self.layers) * 2 + 1 - self.core
        return seq, base + lax.rem(spot, self.layers)

    def each(self, body, near_first=False):
        levels = range(self.layers) if near_first else range(self.layers)[::-1]
        for level in levels:
            layer = lax.rem(self.layer + level, self.layers)

            @pl.loop(0 if level else 1, self.planes)
            def _(step):
                body(lax.rem(self.column + step, self.planes) * self.layers + layer)


def greet(at):
    barrier = pltpu.get_barrier_semaphore()

    def hello(device):
        pl.semaphore_signal(barrier, inc=1, device_id=device, device_id_type=MESH)

    hello(at.opposite)
    at.each(lambda spot: hello(at.peer(spot)))
    hello(at.partner)


class Total:
    def __init__(self, at, blocks, wide, near, sent, out, half, mine, parts, cross, sems):
        self.at, self.blocks, self.wide = at, blocks, wide
        self.piece = cross.shape[1]
        self.near, self.sent, self.out = near, sent, out
        self.half, self.mine, self.parts, self.cross, self.sems = half, mine, parts, cross, sems

    def copy(self, src, dst, send, recv, to):
        return pltpu.make_async_remote_copy(
            src_ref=src,
            dst_ref=dst,
            send_sem=send,
            recv_sem=recv,
            device_id=to,
            device_id_type=MESH,
        )

    def rows(self, spot, side=None):
        base = spot if side is None else side * self.at.group + spot
        return pl.ds(pl.multiple_of(base * self.piece, 16), self.piece)

    def swap(self):
        span = self.at.group * self.piece
        other = pl.ds(pl.multiple_of((1 - self.at.core) * span, 16), span)
        return self.copy(
            self.sent.at[other], self.half, self.sems[0], self.sems[1], self.at.partner
        )

    def scatter(self, spot, slot):
        return self.copy(
            self.mine.at[self.rows(spot)],
            self.parts.at[self.rows(slot)],
            self.sems[2].at[spot],
            self.sems[3].at[slot],
            self.at.peer(spot),
        )

    def exchange(self):
        return [
            self.copy(
                self.cross.at[2],
                self.cross.at[i],
                self.sems[4].at[i],
                self.sems[5].at[i],
                to,
            )
            for i, to in enumerate([self.at.partner, self.at.opposite])
        ]

    def gather(self, spot, slot, side):
        return self.copy(
            self.out.at[self.rows(slot, side)],
            self.out.at[self.rows(slot, side)],
            self.sems[6].at[spot],
            self.sems[7].at[slot],
            self.at.peer(spot),
        )

    def forward(self, spot, side):
        return self.copy(
            self.out.at[self.rows(spot, side)],
            self.out.at[self.rows(spot, side)],
            self.sems[8].at[spot],
            self.sems[9].at[spot],
            self.at.partner,
        )

    def views(self):
        size = self.wide.shape[0]
        for step, block in enumerate(self.blocks):
            yield (
                slice(block * LANES, (block + 1) * LANES),
                slice(step * size, (step + 1) * size),
            )

    def pack(self):
        for cols, rows in self.views():
            lanes = self.wide[:, cols]
            self.near[rows, :] = lanes
            self.sent[rows, :] = lanes.astype(bf16)
        used = self.wide.shape[0] * len(self.blocks)
        left = self.near.shape[0] - used
        if left:
            self.near[used:, :] = jnp.zeros((left, LANES), f32)
            self.sent[used:, :] = jnp.zeros((left, LANES), bf16)

    def spread(self):
        at = self.at

        def one(spot):
            own = self.near[self.rows(spot, at.core), :]
            both = own + self.half[self.rows(spot), :].astype(f32)
            self.mine[self.rows(spot), :] = both.astype(bf16)
            self.scatter(spot, at.spot).start()

        at.each(one)
        one(at.spot)

    def reduce(self):
        at = self.at

        def add(spot):
            self.scatter(spot, spot).wait_recv()
            self.near[: self.piece, :] += self.parts[self.rows(spot), :].astype(f32)

        self.scatter(at.spot, at.spot).wait_recv()
        self.near[: self.piece, :] = self.parts[self.rows(at.spot), :].astype(f32)
        at.each(add, near_first=True)
        self.cross[2] = self.near[: self.piece, :].astype(bf16)
        for copy in self.exchange()[::-1]:
            copy.start()

    def settle(self):
        at = self.at
        for copy in self.exchange():
            copy.wait_recv()
        both = self.cross[0].astype(f32) + self.cross[1].astype(f32)
        self.out[self.rows(at.spot, at.core), :] = both.astype(bf16)

        def one(spot):
            self.gather(spot, at.spot, at.core).start()

        at.each(one)
        one(at.spot)

    def relay(self):
        side = 1 - self.at.core

        def one(spot):
            self.gather(spot, spot, side).wait_recv()
            self.forward(spot, side).start()

        self.at.each(one, near_first=True)
        self.gather(self.at.spot, self.at.spot, side).wait_recv()

    def arrive(self, result):
        at = self.at
        at.each(lambda spot: self.forward(spot, at.core).wait_recv(), near_first=True)
        for cols, rows in self.views():
            result[:, cols] = self.out[rows, :].astype(result.dtype)

    def drain(self):
        at = self.at
        self.swap().wait_send()

        def one(spot):
            self.scatter(spot, at.spot).wait_send()
            self.gather(spot, at.spot, at.core).wait_send()

        def other(spot):
            one(spot)
            self.forward(spot, 1 - at.core).wait_send()

        at.each(other)
        one(at.spot)
        for copy in self.exchange():
            copy.wait_send()


def kept_tokens(tok, first, clip_ref, flags_ref):
    token = lax.broadcasted_iota(jnp.int32, (8, tok), 1)
    kept = jnp.zeros((8, tok), jnp.int32)
    for block in range(tok // BLK):
        inside = (token >= block * BLK) & (token < (block + 1) * BLK)
        kept = jnp.where(inside, flags_ref[block], kept)
    before = token + first < clip_ref[0]
    return jnp.where(before & (kept == 1), 1.0, 0.0).astype(f32)[:1]


def step_kernel(
    chips, depth, spans,
    q_hbm, k_hbm, v_hbm, qt_hbm, kt_hbm, vt_hbm, t_hbm, w_hbm, gain_hbm, clip_hbm, flags_hbm,
    res_ref, gq_ref, grad_ref, k, v, valid_ref,
    q, qt, kt, vt, teach, weight, gain_ref, clip_ref, flags_ref, loads,
    flat, flat_dot, part, unnorm, scale, normed, ngrad, ugrad, turned, gain,
    *rest,
):
    at = Where(chips, depth)
    greet(at)
    tok = q.shape[1]
    pairs = [
        (k_hbm, k),
        (v_hbm, v),
        (clip_hbm, clip_ref),
        (flags_hbm, flags_ref),
        (kt_hbm, kt),
        (vt_hbm, vt),
        (w_hbm, weight),
        (q_hbm, q),
        (qt_hbm, qt),
        (gain_hbm, gain_ref),
        (t_hbm, teach),
    ]
    incoming = [pltpu.make_async_copy(*pair, loads.at[i]) for i, pair in enumerate(pairs)]
    for load in incoming[:6]:
        load.start()
    wides = rest[:3]
    bufs, sems = rest[3 : 3 + 7 * len(spans)], rest[3 + 7 * len(spans) :]
    state, state_dot, early, late = (
        Total(
            at, span, wides[min(i, 2)], *bufs[7 * i : 7 * i + 7], sems[10 * i : 10 * i + 10]
        )
        for i, span in enumerate(spans)
    )
    lead = -(-len(early.blocks) * LANES // E)

    def head(ref, h):
        return ref[h * E : (h + 1) * E, :]

    def cols(h):
        return slice(h * E, (h + 1) * E)

    for wide in wides:
        edge = wide.shape[1] - LANES
        wide[:, edge:] = jnp.zeros((wide.shape[0], LANES), f32)
    for load in incoming[:4]:
        load.wait()
    for load in incoming[6:]:
        load.start()
    device = lax.axis_index("seq") * depth + at.sub
    valid = kept_tokens(tok, device * tok, clip_ref, flags_ref)
    valid_ref[...] = jnp.broadcast_to(valid, valid_ref.shape)
    for h in range(H):
        feat = (jnp.maximum(head(k, h).astype(f32), 0.0) * valid).astype(bf16)
        ugrad[cols(h), :] = feat
        state.wide[:, cols(h)] = dot(head(v, h), feat, (1, 1))
    state.pack()
    pl.semaphore_wait(pltpu.get_barrier_semaphore(), at.group + 1)
    state.swap().start()
    for load in incoming[4:6]:
        load.wait()
    for h in range(H):
        slope = jnp.where(head(k, h).astype(f32) > 0, 1.0, 0.0) * valid
        along = (slope * head(kt, h).astype(f32)).astype(bf16)
        state_dot.wide[:, cols(h)] = dot(head(v, h), along, (1, 1)) + dot(
            head(vt, h), head(ugrad, h), (1, 1)
        )
    state_dot.pack()
    state_dot.swap().start()
    state.swap().wait_recv()
    state.spread()
    state_dot.swap().wait_recv()
    state_dot.spread()

    for load in incoming[6:]:
        load.wait()
    row = lax.broadcasted_iota(jnp.int32, (E, E), 0)
    col = lax.broadcasted_iota(jnp.int32, (E, E), 1)
    for h in range(H):
        spread = jnp.where(row == col, gain_ref[cols(h)][None, :], 0.0)
        gain[cols(h), :] = jnp.sum(spread, axis=1, keepdims=True)
    for start in range(0, weight.shape[1], 256):
        stop = min(start + 256, weight.shape[1])
        turned[start:stop, :] = weight[:, start:stop].T

    state.reduce()
    state_dot.reduce()
    state.settle()
    state_dot.settle()

    def query(h):
        rows = head(q, h).astype(f32)
        return jnp.maximum(rows, 0.0).astype(bf16), jnp.where(rows > 0, 1.0, 0.0).astype(f32)

    state.relay()
    state_dot.relay()
    state.arrive(flat)
    for h in range(H):
        feat, slope = query(h)
        along = (slope * head(qt, h).astype(f32)).astype(bf16)
        matrix = flat[:, cols(h)]
        un = dot(matrix, feat, (1, 0))
        unnorm[cols(h), :] = un
        scale[h] = lax.rsqrt(jnp.mean(un * un, axis=0, keepdims=True) + 1e-06)
        part[cols(h), :] = dot(matrix, along, (1, 0))
    state_dot.arrive(flat_dot)
    for h in range(H):
        un_dot = head(part, h) + dot(flat_dot[:, cols(h)], query(h)[0], (1, 0))
        back = norm_back(head(unnorm, h), scale[h], un_dot)
        normed[cols(h), :] = (gain[cols(h), :] * back).astype(bf16)

    velocity = dot(turned[...], normed[...], (1, 0))
    res_ref[...] = (velocity - teach[...].astype(f32)).astype(bf16)

    def grads(first, last):
        rows = slice(first * E, last * E)
        ngrad[rows, :] = dot(weight[rows, :], res_ref[...], (1, 0))
        for h in range(first, last):
            weighted = gain[cols(h), :] * head(ngrad, h)
            grad = norm_back(head(unnorm, h), scale[h], weighted).astype(bf16)
            ugrad[cols(h), :] = grad
            early.wide[:, cols(h)] = dot(grad, query(h)[0], (1, 1))

    grads(0, lead)
    early.pack()
    early.swap().start()
    grads(lead, H)
    late.pack()
    late.swap().start()
    early.swap().wait_recv()
    early.spread()
    late.swap().wait_recv()
    late.spread()
    for h in range(H):
        back = dot(flat[:, cols(h)], head(ugrad, h), (0, 0))
        gq_ref[cols(h), :] = (query(h)[1] * back).astype(bf16)
    state.drain()
    state_dot.drain()
    early.reduce()
    late.reduce()
    early.settle()
    late.settle()
    early.relay()
    late.relay()
    early.arrive(grad_ref)
    late.arrive(grad_ref)
    early.drain()
    late.drain()


def finish_kernel(
    k, v, res, gq, grad_ref, valid_ref,
    res_out, gq_out, gk_out, gv_out,
    gk, gv, stores,
):
    whole = [
        pltpu.make_async_copy(src, dst, stores.at[2 * H + i])
        for i, (src, dst) in enumerate([(res, res_out), (gq, gq_out)])
    ]
    for store in whole:
        store.start()
    valid = valid_ref[:1, :]
    outgoing = []
    for h in range(H):
        rows = slice(h * E, (h + 1) * E)
        total = grad_ref[:, rows]
        keys = k[rows, :].astype(f32)
        slope = jnp.where(keys > 0, 1.0, 0.0) * valid
        feat = (jnp.maximum(keys, 0.0) * valid).astype(bf16)
        gk[rows, :] = (slope * dot(total, v[rows, :], (0, 0))).astype(bf16)
        gv[rows, :] = dot(total, feat, (1, 0)).astype(bf16)
        for i, (src, dst) in enumerate([(gk, gk_out), (gv, gv_out)]):
            outgoing.append(
                pltpu.make_async_copy(src.at[rows], dst.at[rows], stores.at[2 * h + i])
            )
            outgoing[-1].start()
    for store in whole + outgoing:
        store.wait()


def local(
    query_rows,
    key_rows,
    value_rows,
    query_tangent,
    key_tangent,
    value_tangent,
    teacher,
    out_weight,
    norm_gain,
    clip_length,
    block_mask,
):
    tok, width = query_rows.shape
    depth = lax.axis_size("sub")
    chips = lax.axis_size("seq") // 2 * depth
    padded = -(-width // LANES) * LANES
    vmem = pltpu.VMEM
    dma = pltpu.SemaphoreType.DMA
    group = chips // 2
    group = chips // 2
    blocks = padded // LANES
    cut = -(-blocks // 2)
    spans = [range(blocks)] * 2 + [range(cut), range(cut, blocks)]
    totals = [vmem((E, padded), f32)] * 3
    for span in spans:
        piece = -(-(E * len(span)) // (32 * group)) * 16
        half = (group * piece, LANES)
        full = (2 * group * piece, LANES)
        totals += [vmem(full, f32), vmem(full, bf16), vmem(full, bf16)]
        totals += [vmem(half, bf16)] * 3 + [vmem((3, piece, LANES), bf16)]
    arrays = (query_rows, key_rows, value_rows, query_tangent, key_tangent, value_tangent)
    arrays = tuple(array.T for array in arrays + (teacher,)) + (out_weight,)
    anywhere = pl.BlockSpec(memory_space=pltpu.HBM)
    in_vmem = pl.BlockSpec(memory_space=vmem)
    wide_t = jax.ShapeDtypeStruct((width, tok), bf16)
    res_t = jax.ShapeDtypeStruct(teacher.shape[::-1], bf16)
    handed = [(res_t.shape, bf16), (wide_t.shape, bf16), ((E, padded), bf16)]
    handed += [(wide_t.shape, bf16)] * 2 + [((8, tok), f32)]
    held = sum(rows * cols * jnp.dtype(kind).itemsize for (rows, cols), kind in handed)
    res, grad_query, grad, keys, values, valid = pl.pallas_call(
        functools.partial(step_kernel, chips, depth, spans),
        out_shape=[vmem(*piece) for piece in handed],
        in_specs=[anywhere] * 11,
        out_specs=[in_vmem] * 6,
        scratch_shapes=[vmem(arrays[i].shape, bf16) for i in (0, 3, 4, 5, 6, 7)]
        + [vmem(norm_gain.shape, f32)]
        + [pltpu.SMEM(array.shape, jnp.int32) for array in (clip_length, block_mask)]
        + [dma((11,))]
        + [
            vmem((E, padded), bf16),
            vmem((E, padded), bf16),
            vmem((width, tok), f32),
            vmem((width, tok), f32),
            vmem((H, 1, tok), f32),
            vmem((width, tok), bf16),
            vmem((width, tok), f32),
            vmem((width, tok), bf16),
            vmem(out_weight.shape[::-1], bf16),
            vmem((width, 1), f32),
        ]
        + totals
        + ([dma, dma] + [dma((group,))] * 2 + [dma((2,))] * 2 + [dma((group,))] * 4) * len(spans),
        compiler_params=pltpu.CompilerParams(
            collective_id=0, has_side_effects=True, vmem_limit_bytes=VMEM_BYTES - held
        ),
    )(*arrays, norm_gain, clip_length, block_mask)
    outs = pl.pallas_call(
        finish_kernel,
        out_shape=(res_t, wide_t, wide_t, wide_t),
        in_specs=[in_vmem] * 6,
        out_specs=[anywhere] * 4,
        scratch_shapes=[vmem(wide_t.shape, bf16)] * 2 + [dma((2 * H + 2,))],
        compiler_params=pltpu.CompilerParams(vmem_limit_bytes=FINISH_VMEM),
    )(keys, values, res, grad_query, grad, valid)
    return tuple(out.T for out in outs)


def solution(mesh):
    return jax.shard_map(
        local,
        mesh=mesh,
        in_specs=(
            P(("seq", "sub"), None),
            P(("seq", "sub"), None),
            P(("seq", "sub"), None),
            P(("seq", "sub"), None),
            P(("seq", "sub"), None),
            P(("seq", "sub"), None),
            P(("seq", "sub"), None),
            P(),
            P(),
            P(),
            P(("seq", "sub")),
        ),
        out_specs=(
            P(("seq", "sub"), None),
            P(("seq", "sub"), None),
            P(("seq", "sub"), None),
            P(("seq", "sub"), None),
        ),
        check_vma=False,
    )
```
